32 devices in a mesh: ctx: 8 (over z, y), ch: 4 (over x, core).
Axes of the slice: x: 2, y: 2, z: 4, core: 2. Of those that a mesh axis runs over, the one named last changes fastest.
Arguments:
- query: bfloat16 [32768, 512], P('ctx', 'ch'), parts along dimension 1, may hold values from -6 to 6
- key_proj: bfloat16 [32768, 512], P('ctx', 'ch'), parts along dimension 1, may hold values from -6 to 6
- value: bfloat16 [32768, 512], P('ctx', 'ch'), parts along dimension 1, may hold values from -6 to 6
- short_taps: float32 [3, 3, 512], P(None, None, 'ch'), parts along dimension 2, may hold values from -3.5 to 3.5
- bias: float32 [512], P('ch'), parts along dimension 0, may hold values from -4 to 4
- long_filter: bfloat16 [32768, 512], P('ctx', 'ch'), parts along dimension 1, may hold values from -0.03125 to 0.03125
Outputs:
- gated: bfloat16 [32768, 512], P('ctx', 'ch'), parts along dimension 1
The draws below stay inside these ranges and needn't reach their ends.
There are 4 independent parts, one for each index of `ch`. The reference program is written for one: setup_inputs(seed, part) draws one part's arguments, and reference() takes and returns one part's arrays. A program takes and returns all parts, laid end to end along the dimension named above; each array names one. Nothing has to cross between parts.
All inputs are finite; a program needn't handle non-finite values.
Results may differ from the reference program's by a relative error of at most 0.006.
Values may be sent and summed in bfloat16 or wider, within the bound.
A program may use at most 128 MiB of HBM per device.

```python
import jax
import jax.numpy as jnp
from jax import lax

C = 128
SHORT = 3
SEQ = 32768


def block_levels(stream_key, shape, cuts, low, largest):
    level, own = 1.0, jax.random.fold_in(stream_key, 6)
    for position, parts in cuts:
        draws = jnp.exp(jax.random.uniform(jax.random.fold_in(own, position), (parts,), jnp.float32, low / len(cuts), largest / len(cuts)))
        level = level * jnp.repeat(draws, shape[position] // parts).reshape([-1 if axis == position else 1 for axis in range(len(shape))])
    return level


def bell_draw(key, extent, spread, bound, pieces=(), held_as=jnp.bfloat16):
    array = spread * jax.random.normal(key, extent, jnp.float32)
    if pieces:
        array = array * block_levels(key, extent, pieces, -0.22, 0.18)
    return jnp.clip(array, -bound, bound).astype(held_as)


def setup_inputs(seed: int = 0, part: int = 0) -> dict:
    splits = jax.random.split(jax.random.key(seed), 7)
    part_splits = jax.random.split(jax.random.fold_in(splits[6], part), 7)
    return {
        "query": bell_draw(part_splits[0], (SEQ, C), 1.0, 6.0, ((0, 8),)),
        "key_proj": bell_draw(part_splits[1], (SEQ, C), 1.0, 6.0, ((0, 8),)),
        "value": bell_draw(part_splits[2], (SEQ, C), 1.0, 6.0, ((0, 8),)),
        "short_taps": bell_draw(part_splits[3], (3, SHORT, C), SHORT ** -0.5, 3.5, (), jnp.float32),
        "bias": bell_draw(part_splits[4], (C,), 1.0, 4.0, (), jnp.float32),
        "long_filter": bell_draw(part_splits[5], (SEQ, C), SEQ ** -0.5, 0.03125, ((0, 8),)),
    }


def featurize(stream, taps):
    width = stream.shape[1]
    padded = jnp.concatenate([jnp.zeros((SHORT - 1, width), stream.dtype), stream], axis=0)
    total = jnp.zeros(stream.shape, jnp.float32)
    for offset in range(SHORT):
        total = total + taps[offset] * padded[SHORT - 1 - offset:SHORT - 1 - offset + SEQ].astype(jnp.float32)
    return total


def reference(query, key_proj, value, short_taps, bias, long_filter):
    query_feat = featurize(query, short_taps[0]).astype(jnp.bfloat16)
    query_wide = lax.optimization_barrier(query_feat).astype(jnp.float32)
    mixed = (featurize(key_proj, short_taps[1]) * featurize(value, short_taps[2])).astype(jnp.bfloat16)
    mixed_wide = lax.optimization_barrier(mixed).astype(jnp.float32)
    filter_wide = long_filter.astype(jnp.float32)
    spectrum = jnp.fft.rfft(mixed_wide, n=2 * SEQ, axis=0) * jnp.fft.rfft(filter_wide, n=2 * SEQ, axis=0)
    convolved = jnp.fft.irfft(spectrum, n=2 * SEQ, axis=0)[:SEQ].astype(jnp.bfloat16)
    convolved = lax.optimization_barrier(convolved).astype(jnp.float32)
    return (query_wide * (convolved + bias * mixed_wide)).astype(jnp.bfloat16)
```

```python
import functools

import jax
import jax.numpy as jnp
import numpy as np
from jax import lax
from jax.experimental import pallas as pl
from jax.experimental.pallas import tpu as pltpu
from jax.sharding import PartitionSpec as P

BF = jnp.bfloat16
F32 = jnp.float32
ROWS = 32


def halves(table):
    table = np.asarray(table, np.float32)
    high = table.astype(jnp.bfloat16)
    return high, (table - high.astype(np.float32)).astype(jnp.bfloat16)


def make_tables(parts, length, width):
    group = width // parts
    fine = length // parts
    n = parts * length
    unit = np.arange(parts)
    v = np.arange(fine)
    place = parts * unit[:, None] + np.repeat(unit, group)[None, :]
    phase = place[None] * (unit[:, None, None] + 0.25) / parts**2
    coef = np.exp(-2j * np.pi * phase)
    coef = np.stack([coef.real, coef.imag]).astype(np.float32).reshape(2, parts * parts, width)
    short = np.kron(np.exp(-2j * np.pi * np.outer(unit, unit) / parts), np.eye(group))
    short = np.block([[short.real, short.imag], [-short.imag, short.real]])
    lane = np.exp(-2j * np.pi * np.outer(v, np.repeat(unit, group)) * parts / n)
    column = np.exp(-2j * np.pi * np.outer(v, unit + 0.25) / n)
    inner = np.exp(-2j * np.pi * (np.outer(v, v) % fine) / fine)
    c_h, c_l = halves(inner.real)
    s_h, s_l = halves(-inner.imag)

    def block(c, s):
        c, s = jnp.asarray(c), jnp.asarray(s)
        return jnp.concatenate(
            [jnp.concatenate([c, s], axis=1), jnp.concatenate([-s, c], axis=1)], axis=0
        )

    cr, ci = column.real.astype(np.float32).T[:, :, None], column.imag.astype(np.float32).T[:, :, None]
    lr, li = lane.real.astype(np.float32)[None], lane.imag.astype(np.float32)[None]
    spin = jnp.stack([cr * lr - ci * li, cr * li + ci * lr])
    short_h, short_l = halves(short)
    return coef, short_h, short_l, spin, block(c_h, s_h), block(c_l, s_l)


def dot(a, b):
    return jnp.dot(a, b, preferred_element_type=F32)


def split(value):
    high = value.astype(BF)
    return high, (value - high.astype(F32)).astype(BF)


def regroup(source, target, parts, fine, width):
    group = width // parts
    rows = min(fine, 128)
    lane = lax.broadcasted_iota(jnp.int32, (rows, width), 1) // group

    def step(i, carry):
        at = pl.ds(pl.multiple_of(i * rows, rows), rows)
        loaded = [source(w, at).astype(F32) for w in range(parts)]
        for d in range(parts):
            total = jnp.zeros((rows, width), F32)
            for w in range(parts):
                shift = ((w - d) % parts) * group
                moved = pltpu.roll(loaded[w], shift, 1) if shift else loaded[w]
                total = jnp.where(lane == w, moved, total)
            target(d, at, total.astype(BF))
        return carry

    lax.fori_loop(0, fine // rows, step, 0)


def pack_kernel(parts, fine, width, x_ref, o_ref):
    def load(w, at):
        return x_ref[w, at, :]

    def store(d, at, value):
        o_ref[d, at, :] = value

    regroup(load, store, parts, fine, width)


def forward(parts, fine, width, x_ref, coef, short_h, short_l, spin, big_h, big_l, z_h, z_l, y_h, y_l, finish):
    def first(i, carry):
        at = pl.ds(pl.multiple_of(i * ROWS, ROWS), ROWS)
        xs = [x_ref[j, at, :].astype(F32) for j in range(parts)]
        for a in range(parts):
            re = xs[0] * coef[0, a * parts][None]
            im = xs[0] * coef[1, a * parts][None]
            for j in range(1, parts):
                re = re + xs[j] * coef[0, a * parts + j][None]
                im = im + xs[j] * coef[1, a * parts + j][None]
            re_h, re_l = split(re)
            im_h, im_l = split(im)
            z_h[a, at, 0:width] = re_h
            z_l[a, at, 0:width] = re_l
            z_h[a, at, width:] = im_h
            z_l[a, at, width:] = im_l
        return carry

    lax.fori_loop(0, fine // ROWS, first, 0)

    def pair(p, carry):
        for e in range(2):
            a = 2 * p + e
            high = z_h[a]
            t = dot(high, short_h[...]) + dot(high, short_l[...]) + dot(z_l[a], short_h[...])
            re, im = t[:, :width], t[:, width:]
            sr, si = spin[0, a], spin[1, a]
            re_h, re_l = split(re * sr - im * si)
            im_h, im_l = split(re * si + im * sr)
            cols = slice(e * width, (e + 1) * width)
            y_h[0:fine, cols] = re_h
            y_l[0:fine, cols] = re_l
            y_h[fine:, cols] = im_h
            y_l[fine:, cols] = im_l
        high = y_h[...]
        out = dot(big_h[...], high) + dot(big_l[...], high) + dot(big_h[...], y_l[...])
        finish(p, out)
        return carry

    lax.fori_loop(0, parts // 2, pair, 0)


def filter_kernel(parts, fine, width, x_ref, coef, short_h, short_l, spin, big_h, big_l, o_ref, z_h, z_l, y_h, y_l):
    def finish(p, out):
        o_ref[p] = out

    forward(parts, fine, width, x_ref, coef, short_h, short_l, spin, big_h, big_l, z_h, z_l, y_h, y_l, finish)


def main_kernel(
    parts, fine, width, x_ref, h_ref, coef, short_h, short_l, spin, big_h, big_l, o_ref, z_h, z_l, y_h, y_l, u
):
    scale = float(1.0 / (parts * parts * fine))

    def finish(p, out):
        xr, xi = out[:fine], out[fine:]
        hr, hi = h_ref[p, 0:fine], h_ref[p, fine:]
        y_h[0:fine] = (xr * hr - xi * hi).astype(BF)
        y_h[fine:] = (-(xr * hi + xi * hr)).astype(BF)
        back = dot(big_h[...], y_h[...])
        for e in range(2):
            a = 2 * p + e
            cols = slice(e * width, (e + 1) * width)
            zr, zi = back[:fine, cols], -back[fine:, cols]
            sr, si = spin[0, a], spin[1, a]
            turned = jnp.concatenate([zr * sr + zi * si, zi * sr - zr * si], axis=1).astype(BF)
            u[a] = lax.dot_general(
                turned, short_h[...], (((1,), (1,)), ((), ())), preferred_element_type=F32
            )

    forward(parts, fine, width, x_ref, coef, short_h, short_l, spin, big_h, big_l, z_h, z_l, y_h, y_l, finish)

    def last(i, carry):
        at = pl.ds(pl.multiple_of(i * ROWS, ROWS), ROWS)
        for j in range(parts):
            total = jnp.zeros((ROWS, width), F32)
            for a in range(parts):
                total = total + u[a, at, 0:width] * coef[0, a * parts + j][None]
                total = total + u[a, at, width:] * coef[1, a * parts + j][None]
            o_ref[j, at, :] = (total * scale).astype(BF)
        return carry

    lax.fori_loop(0, fine // ROWS, last, 0)


def from_behind(block, axis, distance):
    devices = range(lax.axis_size(axis))
    route = [(i - distance, i) for i in devices if i - distance in devices]
    return lax.ppermute(block, axis, route)


def featurize(stream, before, taps):
    length = stream.shape[0]
    count = taps.shape[0]
    extended = jnp.concatenate([before, stream], axis=0)
    total = jnp.zeros(stream.shape, F32)
    for offset in range(count):
        total = total + taps[offset] * extended[count - 1 - offset : count - 1 - offset + length].astype(F32)
    return total


def local(query, key_proj, value, short_taps, bias, long_filter):
    length, width = query.shape
    parts = lax.axis_size("ctx")
    fine = length // parts
    keep = short_taps.shape[1] - 1
    tables = make_tables(parts, length, width)
    shape = (parts, fine, width)
    params = pltpu.CompilerParams(vmem_limit_bytes=56 * 1024 * 1024)
    scratch = [
        pltpu.VMEM((parts, fine, 2 * width), BF),
        pltpu.VMEM((parts, fine, 2 * width), BF),
        pltpu.VMEM((2 * fine, 2 * width), BF),
        pltpu.VMEM((2 * fine, 2 * width), BF),
    ]
    flops = 2 * 3 * parts * fine * (4 * width * width + 4 * fine * width)

    def call(body, out, scratch_shapes, work, *args):
        return pl.pallas_call(
            functools.partial(body, parts, fine, width),
            out_shape=out,
            scratch_shapes=scratch_shapes,
            compiler_params=params,
            cost_estimate=pl.CostEstimate(flops=work, bytes_accessed=8 << 20, transcendentals=0),
        )(*args)

    packed = jax.ShapeDtypeStruct(shape, BF)

    def pack(rows):
        return call(pack_kernel, packed, [], 1 << 20, rows.reshape(shape))

    def exchange(blocks):
        return lax.all_to_all(blocks, "ctx", split_axis=0, concat_axis=0, tiled=True)

    gathered_filter = exchange(pack(long_filter))
    edges = jnp.stack([query[length - keep :], key_proj[length - keep :], value[length - keep :]])
    before = from_behind(edges, "ctx", 1)
    query_feat = featurize(query, before[0], short_taps[0]).astype(BF)
    query_wide = lax.optimization_barrier(query_feat).astype(F32)
    mixed = (featurize(key_proj, before[1], short_taps[1]) * featurize(value, before[2], short_taps[2])).astype(BF)
    gathered = exchange(pack(mixed))
    spectrum = call(
        filter_kernel,
        jax.ShapeDtypeStruct((parts // 2, 2 * fine, 2 * width), F32),
        scratch,
        flops,
        gathered_filter,
        *tables,
    )
    rows = call(
        main_kernel,
        packed,
        scratch + [pltpu.VMEM((parts, fine, 2 * width), F32)],
        2 * flops,
        gathered,
        spectrum,
        *tables,
    )
    convolved = pack(exchange(rows)).reshape(length, width).astype(F32)
    return (query_wide * (convolved + bias * mixed.astype(F32))).astype(BF)


def solution(mesh):
    in_specs = (
        P("ctx", "ch"),
        P("ctx", "ch"),
        P("ctx", "ch"),
        P(None, None, "ch"),
        P("ch"),
        P("ctx", "ch"),
    )
    return jax.shard_map(local, mesh=mesh, in_specs=in_specs, out_specs=P("ctx", "ch"), check_vma=False)
```

```python
import functools

import jax
import jax.numpy as jnp
import numpy as np
from jax import lax
from jax.experimental import pallas as pl
from jax.experimental.pallas import tpu as pltpu
from jax.sharding import PartitionSpec as P

BF = jnp.bfloat16
F32 = jnp.float32
ROWS = 32
CHUNKS = 2
MESH = pl.DeviceIdType.MESH


def halves(table):
    table = np.asarray(table, np.float32)
    high = table.astype(jnp.bfloat16)
    return high, (table - high.astype(np.float32)).astype(jnp.bfloat16)


def make_tables(parts, fold, length, width):
    group = width // fold
    fine = length // fold
    n = parts * length
    unit = np.arange(parts)
    block = np.arange(fold)
    v = np.arange(fine)
    place = fold * unit[:, None] + np.repeat(block, group)[None, :]
    phase = place[None] * (unit[:, None, None] + 0.25) / (parts * fold)
    coef = np.exp(-2j * np.pi * phase)
    coef = np.stack([coef.real, coef.imag]).astype(np.float32).reshape(2, parts * parts, width)
    short = np.kron(np.exp(-2j * np.pi * np.outer(block, block) / fold), np.eye(group))
    short = np.block([[short.real, short.imag], [-short.imag, short.real]])
    lane = np.exp(-2j * np.pi * np.outer(v, np.repeat(block, group)) * parts / n)
    column = np.exp(-2j * np.pi * np.outer(v, unit + 0.25) / n)
    inner = np.exp(-2j * np.pi * (np.outer(v, v) % fine) / fine)
    big = np.block([[inner.real, -inner.imag], [inner.imag, inner.real]])
    spin = column.T[:, :, None] * lane[None]
    spin = np.stack([spin.real, spin.imag]).astype(np.float32)
    return (coef, *halves(short), spin, *halves(big))


def dot(a, b):
    return jnp.dot(a, b, preferred_element_type=F32)


def split(value):
    high = value.astype(BF)
    return high, (value - high.astype(F32)).astype(BF)


def regroup(xs, fold, width):
    group = width // fold
    lane = lax.broadcasted_iota(jnp.int32, xs[0].shape, 1) // group
    bit = 1
    while bit < fold:
        high = (lane // bit) % 2 == 1
        out = list(xs)
        for i in range(fold):
            if i & bit == 0:
                low_x, high_x = xs[i], xs[i + bit]
                out[i] = jnp.where(high, pltpu.roll(high_x, bit * group, 1), low_x)
                out[i + bit] = jnp.where(high, high_x, pltpu.roll(low_x, width - bit * group, 1))
        xs = out
        bit *= 2
    return xs


def body(
    parts, fold, fine, width,
    q_ref, k_ref, v_ref, taps, bias, f_ref, coef, short_h, short_l, spin, big_h, big_l, o_ref,
    halo, mixed, q_feat, out_f, out_m, out_y, in_f, in_m, in_y,
    z_h, z_l, y_h, y_l, spectrum, u, send, recv, own, halo_send, halo_recv,
):
    me = lax.axis_index("ctx")
    chunks = fold // parts
    length = fold * fine
    scale = float(1.0 / (parts * length))
    count = taps.shape[1]
    streams = (q_ref, k_ref, v_ref)

    barrier = pltpu.get_barrier_semaphore()

    def greet(k, carry):
        pl.semaphore_signal(barrier, inc=1, device_id={"ctx": lax.rem(me + k, parts)}, device_id_type=MESH)
        return carry

    lax.fori_loop(1, parts, greet, 0)

    outs = (out_f, out_m, out_y)
    ins = (in_f, in_m, in_y)

    def remote(kind, g, k):
        there = lax.rem(me + k, parts)
        return pltpu.make_async_remote_copy(
            src_ref=outs[kind].at[g, there],
            dst_ref=ins[kind].at[g, me],
            send_sem=send.at[kind, g, there],
            recv_sem=recv.at[kind, g, me],
            device_id={"ctx": there},
            device_id_type=MESH,
        )

    def arrival(kind, g, k):
        there = lax.rem(me + k, parts)
        return pltpu.make_async_remote_copy(
            src_ref=outs[kind].at[g, there],
            dst_ref=ins[kind].at[g, there],
            send_sem=send.at[kind, g, there],
            recv_sem=recv.at[kind, g, there],
            device_id={"ctx": there},
            device_id_type=MESH,
        )

    def local_copy(kind, g):
        return pltpu.make_async_copy(outs[kind].at[g, me], ins[kind].at[g, me], own.at[kind, g])

    def start(kind, g):
        def go(k, carry):
            remote(kind, g, k).start()
            return carry

        lax.fori_loop(1, parts, go, 0)
        local_copy(kind, g).start()

    def wait(kind, g):
        def go(k, carry):
            arrival(kind, g, k).wait_recv()
            return carry

        lax.fori_loop(1, parts, go, 0)
        local_copy(kind, g).wait()

    def drain(kind, g):
        def go(k, carry):
            remote(kind, g, k).wait_send()
            return carry

        lax.fori_loop(1, parts, go, 0)

    def halo_copy(s):
        return pltpu.make_async_remote_copy(
            src_ref=streams[s].at[pl.ds(length - 16, 16)],
            dst_ref=halo.at[s],
            send_sem=halo_send.at[s],
            recv_sem=halo_recv.at[s],
            device_id={"ctx": lax.rem(me + 1, parts)},
            device_id_type=MESH,
        )

    tile = min(fine, max(16, 512 // fold))

    def pack(x_ref, target):
        def step(i, carry):
            xs = [
                x_ref[pl.ds(pl.multiple_of(w * fine + i * tile, tile), tile), :].astype(F32)
                for w in range(fold)
            ]
            moved = regroup(xs, fold, width)
            at = pl.ds(pl.multiple_of(i * tile, tile), tile)
            for e in range(fold):
                target[e % chunks, e // chunks, at, :] = moved[e].astype(BF)
            return carry

        lax.fori_loop(0, fine // tile, step, 0)

    pack(f_ref, out_f)
    pl.semaphore_wait(barrier, parts - 1)
    for s in range(3):
        halo_copy(s).start()
    for g in range(chunks):
        start(0, g)

    for s in range(3):
        halo_copy(s).wait_recv()
    inside = jnp.where(me == 0, 0.0, 1.0).astype(F32)
    rows = min(length, 64)

    def shifted(x_ref, s, at, tail):
        now = x_ref[at, :].astype(F32)
        extended = jnp.concatenate([tail, now], axis=0)
        total = taps[s, 0][None] * now
        for j in range(1, count):
            total = total + taps[s, j][None] * pltpu.roll(extended, j, 0)[8:]
        return total, now[rows - 8 :]

    tails = [halo[s].astype(F32)[8:] * inside for s in range(3)]

    def features(i, carry):
        at = pl.ds(pl.multiple_of(i * rows, rows), rows)
        key, key_tail = shifted(k_ref, 1, at, carry[0])
        val, val_tail = shifted(v_ref, 2, at, carry[1])
        mixed[at, :] = (key * val).astype(BF)
        return key_tail, val_tail

    lax.fori_loop(0, length // rows, features, (tails[1], tails[2]))
    pack(mixed, out_m)
    for g in range(chunks):
        start(1, g)

    def q_features(i, carry):
        at = pl.ds(pl.multiple_of(i * rows, rows), rows)
        total, tail = shifted(q_ref, 0, at, carry)
        q_feat[at, :] = total.astype(BF)
        return tail

    lax.fori_loop(0, length // rows, q_features, tails[0])

    def forward(x_ref, g, finish):
        def first(i, carry):
            at = pl.ds(pl.multiple_of(i * step_rows, step_rows), step_rows)
            xs = [x_ref[g, j, at, :].astype(F32) for j in range(parts)]
            for a in range(parts):
                re = xs[0] * coef[0, a * parts][None]
                im = xs[0] * coef[1, a * parts][None]
                for j in range(1, parts):
                    re = re + xs[j] * coef[0, a * parts + j][None]
                    im = im + xs[j] * coef[1, a * parts + j][None]
                re_h, re_l = split(re)
                im_h, im_l = split(im)
                z_h[a, at, 0:width] = re_h
                z_l[a, at, 0:width] = re_l
                z_h[a, at, width:] = im_h
                z_l[a, at, width:] = im_l
            return carry

        step_rows = min(fine, ROWS)
        lax.fori_loop(0, fine // step_rows, first, 0)

        def pair(p, carry):
            for e in range(2):
                a = 2 * p + e
                high = z_h[a]
                t = dot(high, short_h[...]) + dot(high, short_l[...]) + dot(z_l[a], short_h[...])
                re, im = t[:, :width], t[:, width:]
                sr, si = spin[0, a], spin[1, a]
                re_h, re_l = split(re * sr - im * si)
                im_h, im_l = split(re * si + im * sr)
                cols = slice(e * width, (e + 1) * width)
                y_h[0:fine, cols] = re_h
                y_l[0:fine, cols] = re_l
                y_h[fine:, cols] = im_h
                y_l[fine:, cols] = im_l
            high = y_h[...]
            out = dot(big_h[...], high) + dot(big_l[...], high) + dot(big_h[...], y_l[...])
            finish(p, out)
            return carry

        lax.fori_loop(0, parts // 2, pair, 0)

    for g in range(chunks):
        wait(0, g)

        def keep(p, out):
            spectrum[g, p] = out

        forward(in_f, g, keep)

    for g in range(chunks):
        wait(1, g)

        def finish(p, out):
            xr, xi = out[:fine], out[fine:]
            hr, hi = spectrum[g, p, 0:fine], spectrum[g, p, fine:]
            y_h[0:fine] = (xr * hr - xi * hi).astype(BF)
            y_h[fine:] = (-(xr * hi + xi * hr)).astype(BF)
            back = dot(big_h[...], y_h[...])
            for e in range(2):
                a = 2 * p + e
                cols = slice(e * width, (e + 1) * width)
                zr, zi = back[:fine, cols], -back[fine:, cols]
                sr, si = spin[0, a], spin[1, a]
                turned = jnp.concatenate([zr * sr + zi * si, zi * sr - zr * si], axis=1).astype(BF)
                u[a] = lax.dot_general(
                    turned, short_h[...], (((1,), (1,)), ((), ())), preferred_element_type=F32
                )

        forward(in_m, g, finish)
        step_rows = min(fine, ROWS)

        def last(i, carry):
            at = pl.ds(pl.multiple_of(i * step_rows, step_rows), step_rows)
            for j in range(parts):
                total = jnp.zeros((step_rows, width), F32)
                for a in range(parts):
                    total = total + u[a, at, 0:width] * coef[0, a * parts + j][None]
                    total = total + u[a, at, width:] * coef[1, a * parts + j][None]
                out_y[g, j, at, :] = (total * scale).astype(BF)
            return carry

        lax.fori_loop(0, fine // step_rows, last, 0)
        start(2, g)

    for g in range(chunks):
        wait(2, g)

    def gate(i, carry):
        at = pl.ds(pl.multiple_of(i * tile, tile), tile)
        xs = [in_y[e % chunks, e // chunks, at, :].astype(F32) for e in range(fold)]
        moved = regroup(xs, fold, width)
        for w in range(fold):
            here = pl.ds(pl.multiple_of(w * fine + i * tile, tile), tile)
            total = moved[w] + bias[...] * mixed[here, :].astype(F32)
            o_ref[here, :] = (q_feat[here, :].astype(F32) * total).astype(BF)
        return carry

    lax.fori_loop(0, fine // tile, gate, 0)

    for s in range(3):
        halo_copy(s).wait_send()
    for kind in range(3):
        for g in range(chunks):
            drain(kind, g)


def local(query, key_proj, value, short_taps, bias, long_filter):
    length, width = query.shape
    parts = lax.axis_size("ctx")
    chunks = CHUNKS
    fold = parts * chunks
    fine = length // fold
    tables = make_tables(parts, fold, length, width)
    block = pltpu.VMEM((chunks, parts, fine, width), BF)
    wide = pltpu.VMEM((parts, fine, 2 * width), BF)
    tall = pltpu.VMEM((2 * fine, 2 * width), BF)
    rows = pltpu.VMEM((length, width), BF)
    return pl.pallas_call(
        functools.partial(body, parts, fold, fine, width),
        out_shape=jax.ShapeDtypeStruct((length, width), BF),
        in_specs=[pl.BlockSpec(memory_space=pltpu.VMEM)] * 12,
        out_specs=pl.BlockSpec(memory_space=pltpu.VMEM),
        scratch_shapes=[
            pltpu.VMEM((3, 16, width), BF),
            rows, rows,
            block, block, block, block, block, block,
            wide, wide, tall, tall,
            pltpu.VMEM((chunks, parts // 2, 2 * fine, 2 * width), F32),
            pltpu.VMEM((parts, fine, 2 * width), F32),
            pltpu.SemaphoreType.DMA((3, chunks, parts)),
            pltpu.SemaphoreType.DMA((3, chunks, parts)),
            pltpu.SemaphoreType.DMA((3, chunks)),
            pltpu.SemaphoreType.DMA((3,)),
            pltpu.SemaphoreType.DMA((3,)),
        ],
        compiler_params=pltpu.CompilerParams(
            vmem_limit_bytes=56 * 1024 * 1024, collective_id=0, has_side_effects=True
        ),
    )(query, key_proj, value, short_taps, bias.reshape(1, width), long_filter, *tables)


def solution(mesh):
    in_specs = (
        P("ctx", "ch"),
        P("ctx", "ch"),
        P("ctx", "ch"),
        P(None, None, "ch"),
        P("ch"),
        P("ctx", "ch"),
    )
    return jax.shard_map(local, mesh=mesh, in_specs=in_specs, out_specs=P("ctx", "ch"), check_vma=False)
```

```python
import functools

import jax
import jax.numpy as jnp
import numpy as np
from jax import lax
from jax.experimental import pallas as pl
from jax.experimental.pallas import tpu as pltpu
from jax.sharding import PartitionSpec as P

BF = jnp.bfloat16
F32 = jnp.float32
ROWS = 32
CHUNKS = 4
MESH = pl.DeviceIdType.MESH


def halves(table):
    table = np.asarray(table, np.float32)
    high = table.astype(jnp.bfloat16)
    return high, (table - high.astype(np.float32)).astype(jnp.bfloat16)


def make_tables(parts, fold, length, width):
    group = width // fold
    fine = length // fold
    n = parts * length
    unit = np.arange(parts)
    block = np.arange(fold)
    v = np.arange(fine)
    place = fold * unit[:, None] + np.repeat(block, group)[None, :]
    phase = place[None] * (unit[:, None, None] + 0.25) / (parts * fold)
    coef = np.exp(-2j * np.pi * phase)
    coef = np.stack([coef.real, coef.imag]).astype(np.float32).reshape(2, parts * parts, width)
    short = np.kron(np.exp(-2j * np.pi * np.outer(block, block) / fold), np.eye(group))
    short = np.block([[short.real, short.imag], [-short.imag, short.real]])
    lane = np.exp(-2j * np.pi * np.outer(v, np.repeat(block, group)) * parts / n)
    column = np.exp(-2j * np.pi * np.outer(v, unit + 0.25) / n)
    inner = np.exp(-2j * np.pi * (np.outer(v, v) % fine) / fine)
    big = np.block([[inner.real, -inner.imag], [inner.imag, inner.real]])
    spin = column.T[:, :, None] * lane[None]
    spin = np.stack([spin.real, spin.imag]).astype(np.float32)
    return (coef, *halves(short), spin, *halves(big))


def dot(a, b):
    return jnp.dot(a, b, preferred_element_type=F32)


def split(value):
    high = value.astype(BF)
    return high, (value - high.astype(F32)).astype(BF)


def regroup(xs, fold, width):
    group = width // fold
    lane = lax.broadcasted_iota(jnp.int32, xs[0].shape, 1) // group
    bit = 1
    while bit < fold:
        high = (lane // bit) % 2 == 1
        out = list(xs)
        for i in range(fold):
            if i & bit == 0:
                low_x, high_x = xs[i], xs[i + bit]
                out[i] = jnp.where(high, pltpu.roll(high_x, bit * group, 1), low_x)
                out[i + bit] = jnp.where(high, high_x, pltpu.roll(low_x, width - bit * group, 1))
        xs = out
        bit *= 2
    return xs


def body(
    parts, fold, fine, width,
    q_ref, k_ref, v_ref, taps, bias, f_ref, coef, short_h, short_l, spin, big_h, big_l, o_ref,
    halo, mixed, q_feat, out_f, out_m, out_y, in_f, in_m, in_y,
    z_h, z_l, y_h, y_l, spectrum, u, send, recv, own, halo_send, halo_recv,
):
    me = lax.axis_index("ctx")
    chunks = fold // parts
    length = fold * fine
    scale = float(1.0 / (parts * length))
    count = taps.shape[1]
    streams = (q_ref, k_ref, v_ref)

    barrier = pltpu.get_barrier_semaphore()

    def greet(k, carry):
        pl.semaphore_signal(barrier, inc=1, device_id={"ctx": lax.rem(me + k, parts)}, device_id_type=MESH)
        return carry

    lax.fori_loop(1, parts, greet, 0)

    outs = (out_f, out_m, out_y)
    ins = (in_f, in_m, in_y)

    def remote(kind, g, k):
        there = lax.rem(me + k, parts)
        return pltpu.make_async_remote_copy(
            src_ref=outs[kind].at[g, there],
            dst_ref=ins[kind].at[g, me],
            send_sem=send.at[kind, g, there],
            recv_sem=recv.at[kind, g, me],
            device_id={"ctx": there},
            device_id_type=MESH,
        )

    def arrival(kind, g, k):
        there = lax.rem(me + k, parts)
        return pltpu.make_async_remote_copy(
            src_ref=outs[kind].at[g, there],
            dst_ref=ins[kind].at[g, there],
            send_sem=send.at[kind, g, there],
            recv_sem=recv.at[kind, g, there],
            device_id={"ctx": there},
            device_id_type=MESH,
        )

    def local_copy(kind, g):
        return pltpu.make_async_copy(outs[kind].at[g, me], ins[kind].at[g, me], own.at[kind, g])

    def start(kind, g):
        def go(k, carry):
            remote(kind, g, k).start()
            return carry

        lax.fori_loop(1, parts, go, 0)
        local_copy(kind, g).start()

    def wait(kind, g):
        def go(k, carry):
            arrival(kind, g, k).wait_recv()
            return carry

        lax.fori_loop(1, parts, go, 0)
        local_copy(kind, g).wait()

    def drain(kind, g):
        def go(k, carry):
            remote(kind, g, k).wait_send()
            return carry

        lax.fori_loop(1, parts, go, 0)

    def halo_copy(s):
        return pltpu.make_async_remote_copy(
            src_ref=streams[s].at[pl.ds(length - 16, 16)],
            dst_ref=halo.at[s],
            send_sem=halo_send.at[s],
            recv_sem=halo_recv.at[s],
            device_id={"ctx": lax.rem(me + 1, parts)},
            device_id_type=MESH,
        )

    tile = min(fine, max(16, 512 // fold))

    def pack(x_ref, target):
        def step(i, carry):
            xs = [
                x_ref[pl.ds(pl.multiple_of(w * fine + i * tile, tile), tile), :].astype(F32)
                for w in range(fold)
            ]
            moved = regroup(xs, fold, width)
            at = pl.ds(pl.multiple_of(i * tile, tile), tile)
            for e in range(fold):
                target[e % chunks, e // chunks, at, :] = moved[e].astype(BF)
            return carry

        lax.fori_loop(0, fine // tile, step, 0)

    pack(f_ref, out_f)
    pl.semaphore_wait(barrier, parts - 1)
    for s in range(3):
        halo_copy(s).start()
    for g in range(chunks):
        start(0, g)

    for s in range(3):
        halo_copy(s).wait_recv()
    inside = jnp.where(me == 0, 0.0, 1.0).astype(F32)
    rows = min(length, 64)

    def shifted(x_ref, s, at, tail):
        now = x_ref[at, :].astype(F32)
        extended = jnp.concatenate([tail, now], axis=0)
        total = taps[s, 0][None] * now
        for j in range(1, count):
            total = total + taps[s, j][None] * pltpu.roll(extended, j, 0)[8:]
        return total, now[rows - 8 :]

    tails = [halo[s].astype(F32)[8:] * inside for s in range(3)]

    def features(i, carry):
        at = pl.ds(pl.multiple_of(i * rows, rows), rows)
        key, key_tail = shifted(k_ref, 1, at, carry[0])
        val, val_tail = shifted(v_ref, 2, at, carry[1])
        mixed[at, :] = (key * val).astype(BF)
        return key_tail, val_tail

    lax.fori_loop(0, length // rows, features, (tails[1], tails[2]))
    pack(mixed, out_m)
    for g in range(chunks):
        start(1, g)

    def q_features(i, carry):
        at = pl.ds(pl.multiple_of(i * rows, rows), rows)
        total, tail = shifted(q_ref, 0, at, carry)
        q_feat[at, :] = total.astype(BF)
        return tail

    lax.fori_loop(0, length // rows, q_features, tails[0])

    def forward(x_ref, g, finish):
        def first(i, carry):
            at = pl.ds(pl.multiple_of(i * step_rows, step_rows), step_rows)
            xs = [x_ref[g, j, at, :].astype(F32) for j in range(parts)]
            for a in range(parts):
                re = xs[0] * coef[0, a * parts][None]
                im = xs[0] * coef[1, a * parts][None]
                for j in range(1, parts):
                    re = re + xs[j] * coef[0, a * parts + j][None]
                    im = im + xs[j] * coef[1, a * parts + j][None]
                re_h, re_l = split(re)
                im_h, im_l = split(im)
                z_h[a, at, 0:width] = re_h
                z_l[a, at, 0:width] = re_l
                z_h[a, at, width:] = im_h
                z_l[a, at, width:] = im_l
            return carry

        step_rows = min(fine, ROWS)
        lax.fori_loop(0, fine // step_rows, first, 0)

        def pair(p, carry):
            for e in range(2):
                a = 2 * p + e
                high = z_h[a]
                t = dot(high, short_h[...]) + dot(high, short_l[...]) + dot(z_l[a], short_h[...])
                re, im = t[:, :width], t[:, width:]
                sr, si = spin[0, a], spin[1, a]
                re_h, re_l = split(re * sr - im * si)
                im_h, im_l = split(re * si + im * sr)
                cols = slice(e * width, (e + 1) * width)
                y_h[0:fine, cols] = re_h
                y_l[0:fine, cols] = re_l
                y_h[fine:, cols] = im_h
                y_l[fine:, cols] = im_l
            high = y_h[...]
            out = dot(big_h[...], high) + dot(big_l[...], high) + dot(big_h[...], y_l[...])
            finish(p, out)
            return carry

        lax.fori_loop(0, parts // 2, pair, 0)

    for g in range(chunks):
        wait(0, g)

        def keep(p, out):
            spectrum[g, p] = out

        forward(in_f, g, keep)

    for g in range(chunks):
        wait(1, g)

        def finish(p, out):
            xr, xi = out[:fine], out[fine:]
            hr, hi = spectrum[g, p, 0:fine], spectrum[g, p, fine:]
            y_h[0:fine] = (xr * hr - xi * hi).astype(BF)
            y_h[fine:] = (-(xr * hi + xi * hr)).astype(BF)
            back = dot(big_h[...], y_h[...])
            for e in range(2):
                a = 2 * p + e
                cols = slice(e * width, (e + 1) * width)
                zr, zi = back[:fine, cols], -back[fine:, cols]
                sr, si = spin[0, a], spin[1, a]
                turned = jnp.concatenate([zr * sr + zi * si, zi * sr - zr * si], axis=1).astype(BF)
                u[a] = lax.dot_general(
                    turned, short_h[...], (((1,), (1,)), ((), ())), preferred_element_type=F32
                )

        forward(in_m, g, finish)
        step_rows = min(fine, ROWS)

        def last(i, carry):
            at = pl.ds(pl.multiple_of(i * step_rows, step_rows), step_rows)
            for j in range(parts):
                total = jnp.zeros((step_rows, width), F32)
                for a in range(parts):
                    total = total + u[a, at, 0:width] * coef[0, a * parts + j][None]
                    total = total + u[a, at, width:] * coef[1, a * parts + j][None]
                out_y[g, j, at, :] = (total * scale).astype(BF)
            return carry

        lax.fori_loop(0, fine // step_rows, last, 0)
        start(2, g)

    for g in range(chunks):
        wait(2, g)

    def gate(i, carry):
        at = pl.ds(pl.multiple_of(i * tile, tile), tile)
        xs = [in_y[e % chunks, e // chunks, at, :].astype(F32) for e in range(fold)]
        moved = regroup(xs, fold, width)
        for w in range(fold):
            here = pl.ds(pl.multiple_of(w * fine + i * tile, tile), tile)
            total = moved[w] + bias[...] * mixed[here, :].astype(F32)
            o_ref[here, :] = (q_feat[here, :].astype(F32) * total).astype(BF)
        return carry

    lax.fori_loop(0, fine // tile, gate, 0)

    for s in range(3):
        halo_copy(s).wait_send()
    for kind in range(3):
        for g in range(chunks):
            drain(kind, g)


def local(query, key_proj, value, short_taps, bias, long_filter):
    length, width = query.shape
    parts = lax.axis_size("ctx")
    chunks = max(1, min(CHUNKS, width // (2 * parts)))
    fold = parts * chunks
    fine = length // fold
    tables = make_tables(parts, fold, length, width)
    block = pltpu.VMEM((chunks, parts, fine, width), BF)
    wide = pltpu.VMEM((parts, fine, 2 * width), BF)
    tall = pltpu.VMEM((2 * fine, 2 * width), BF)
    rows = pltpu.VMEM((length, width), BF)
    return pl.pallas_call(
        functools.partial(body, parts, fold, fine, width),
        out_shape=jax.ShapeDtypeStruct((length, width), BF),
        in_specs=[pl.BlockSpec(memory_space=pltpu.VMEM)] * 12,
        out_specs=pl.BlockSpec(memory_space=pltpu.VMEM),
        scratch_shapes=[
            pltpu.VMEM((3, 16, width), BF),
            rows, rows,
            block, block, block, block, block, block,
            wide, wide, tall, tall,
            pltpu.VMEM((chunks, parts // 2, 2 * fine, 2 * width), F32),
            pltpu.VMEM((parts, fine, 2 * width), F32),
            pltpu.SemaphoreType.DMA((3, chunks, parts)),
            pltpu.SemaphoreType.DMA((3, chunks, parts)),
            pltpu.SemaphoreType.DMA((3, chunks)),
            pltpu.SemaphoreType.DMA((3,)),
            pltpu.SemaphoreType.DMA((3,)),
        ],
        compiler_params=pltpu.CompilerParams(
            vmem_limit_bytes=56 * 1024 * 1024, collective_id=0, has_side_effects=True
        ),
    )(query, key_proj, value, short_taps, bias.reshape(1, width), long_filter, *tables)


def solution(mesh):
    in_specs = (
        P("ctx", "ch"),
        P("ctx", "ch"),
        P("ctx", "ch"),
        P(None, None, "ch"),
        P("ch"),
        P("ctx", "ch"),
    )
    return jax.shard_map(local, mesh=mesh, in_specs=in_specs, out_specs=P("ctx", "ch"), check_vma=False)
```
